1024 devices in a mesh: hi: 64 (over z_lo, y, core), lo: 16 (over x, z_hi).
Axes of the slice: x: 8, y: 8, z: 8 (z_hi: 2, z_lo: 4; z = z_hi * 4 + z_lo), core: 2. Of those that a mesh axis runs over, the one named last changes fastest.
Arguments:
- state: float32 [2, 33554432], P(None, ('hi', 'lo')), may hold values from -15 to 15
- gates: float32 [16, 2, 128, 128], replicated, may hold values from -1 to 1, as said below
- remap_perm: int32 [16], replicated, may hold values from 0 to 15, each once
Outputs:
- final_state: float32 [2, 33554432], P(None, ('hi', 'lo'))
The draws below stay inside these ranges and needn't reach their ends.
Inputs may be any that keep to these rules, and one draw needn't show every extreme that they name: Each gates[g] is a unitary matrix (real part gates[g][0], imaginary part gates[g][1]) up to float32 rounding.
All inputs are finite; a program needn't handle non-finite values.
Results may differ from the reference program's by a relative error of at most 0.00016.
Values sent between devices are 32-bit elements; how exact they have to be, the bound alone decides.
A program may use at most 32 MiB of HBM per device.

```python
import math
import jax
import jax.numpy as jnp
from jax import lax

LOCAL = 32768
GATE = 128
GATES = 16
AMPS = 33554432
N_HI = 64
N_LO = 16


def draw_state(key, part):
    key_values = jax.random.fold_in(key, 21)
    key_block = jax.random.fold_in(key, 22)
    key_global = jax.random.fold_in(key, 23)
    blocks = AMPS // LOCAL
    position = jnp.arange(LOCAL, dtype=jnp.float32) / LOCAL
    local_weight = (1.0 + 3.0 * position) / 4.0
    block_pos = jnp.arange(blocks, dtype=jnp.float32) / blocks
    ramp = (1.0 + 2.0 * (block_pos[:, None] + position[None, :] / blocks)) / 3.0
    block_scale = jnp.exp(jax.random.uniform(key_block, (blocks, 1), jnp.float32, math.log(0.35), 0.0))
    global_scale = jax.random.uniform(key_global, (), jnp.float32, 0.3, 1.0)
    factor = (global_scale * block_scale * ramp * local_weight[None, :]).reshape(AMPS)
    values = jnp.clip(jax.random.normal(key_values, (2, AMPS), jnp.float32), -4.0, 4.0) * 3.5 * factor[None, :]
    return values.astype(jnp.float32)


def draw_gates(key, part):
    key_real = jax.random.fold_in(key, 11)
    key_imag = jax.random.fold_in(key, 12)
    key_perm = jax.random.fold_in(key, 13)
    key_phase = jax.random.fold_in(key, 14)
    matrix = jax.random.normal(key_real, (GATES, GATE, GATE), jnp.float32) + 1j * jax.random.normal(key_imag, (GATES, GATE, GATE), jnp.float32)
    factor_q, factor_r = jnp.linalg.qr(matrix)
    diagonal = jnp.diagonal(factor_r, axis1=1, axis2=2)
    factor_q = factor_q * (diagonal / jnp.abs(diagonal))[:, None, :]
    haar = jnp.stack([jnp.real(factor_q), jnp.imag(factor_q)], axis=1).astype(jnp.float32)
    perms = jax.vmap(lambda single: jax.random.permutation(single, GATE))(jax.random.split(key_perm, GATES))
    columns = jnp.arange(GATE, dtype=jnp.int32)
    permute = (perms[:, :, None] == columns[None, None, :]).astype(jnp.float32)
    phase = jax.random.uniform(key_phase, (GATES, GATE, 1), jnp.float32, -math.pi, math.pi)
    monomial = jnp.stack([permute * jnp.cos(phase), permute * jnp.sin(phase)], axis=1)
    index = jnp.arange(GATES, dtype=jnp.int32)
    chosen = ((index % 4 == 1) | (index % 4 == 2)) & (index < 12)
    return jnp.where(chosen[:, None, None, None], monomial, haar).astype(jnp.float32)


def setup_inputs(seed: int = 0) -> dict:
    key_list = jax.random.split(jax.random.key(seed), 4)
    state = draw_state(jax.random.fold_in(key_list[3], 71), 0)
    gates = draw_gates(jax.random.fold_in(key_list[3], 71), 0)
    remap_perm = jax.random.permutation(key_list[2], N_LO).astype(jnp.int32)
    return {"state": state, "gates": gates, "remap_perm": remap_perm}


def apply_last(blocks, gate):

    def contract(data, matrix):
        return jnp.einsum('...j,ij->...i', data, matrix, precision=lax.Precision.HIGHEST)
    real_out = contract(blocks[0], gate[0]) - contract(blocks[1], gate[1])
    imag_out = contract(blocks[0], gate[1]) + contract(blocks[1], gate[0])
    return jnp.stack([real_out, imag_out])

def apply_mid(blocks, gate):

    def contract(data, matrix):
        return jnp.einsum('ij,ajb->aib', matrix, data, precision=lax.Precision.HIGHEST)
    real_out = contract(blocks[0], gate[0]) - contract(blocks[1], gate[1])
    imag_out = contract(blocks[0], gate[1]) + contract(blocks[1], gate[0])
    return jnp.stack([real_out, imag_out])

def apply_gate(vector, gate, low):
    count = vector.shape[1]
    order = gate.shape[-1]
    if low == 0:
        return apply_last(vector.reshape(2, count // order, order), gate).reshape(2, count)
    width = 1 << low
    shaped = vector.reshape(2, count // (order * width), order, width)
    return apply_mid(shaped, gate).reshape(2, count)

def run_group(vector, gates, group):
    qubits = LOCAL.bit_length() - 1
    gate_bits = gates.shape[-1].bit_length() - 1
    starts = [0, qubits - gate_bits, qubits - gate_bits - 1, 0]
    for layer in range(4):
        vector = apply_gate(vector, gates[4 * group + layer], starts[layer])
    return vector

def swap_ref(vector, bit):
    shaped = vector.reshape(2, N_HI >> bit + 1, 2, (1 << bit) * N_LO, 2, LOCAL // 2)
    return jnp.swapaxes(shaped, 2, 4).reshape(2, -1)

def reference(state, gates, remap_perm):
    top_bit = N_HI.bit_length() - 1
    vector = run_group(state, gates, 0)
    vector = swap_ref(vector, top_bit - 2)
    vector = run_group(vector, gates, 1)
    vector = swap_ref(vector, 0)
    vector = run_group(vector, gates, 2)
    shaped = vector.reshape(2, N_HI, N_LO, N_LO, LOCAL // N_LO)
    moved = jnp.zeros_like(shaped).at[:, :, :, remap_perm].set(shaped)
    vector = jnp.swapaxes(moved, 2, 3).reshape(2, -1)
    vector = run_group(vector, gates, 3)
    vector = swap_ref(vector, top_bit // 2)
    mean_sq = jnp.mean(vector * vector)
    return vector / jnp.sqrt(mean_sq + 1e-06)
```

```python
import functools

import jax
import jax.numpy as jnp
from jax import lax
from jax.experimental import pallas as pl
from jax.experimental.pallas import tpu as pltpu
from jax.sharding import PartitionSpec as P

F32 = jnp.float32
BF16 = jnp.bfloat16
MESH = pl.DeviceIdType.MESH

SWAP_BITS = (4, 0, 3)
NORM_MASKS = [
    (b1 << 1) | (b2 << 2) | (b4 << 4) | (b5 << 5)
    for b5 in (1, 0)
    for b4 in (1, 0)
    for b2 in (1, 0)
    for b1 in (1, 0)
    if b1 or b2 or b4 or b5
]
LO_STEPS = sorted(
    [(dx, dz) for dx in range(8) for dz in range(2) if dx or dz],
    key=lambda s: -(min(s[0], 8 - s[0]) + 4 * s[1]),
)


def bit_of(value, bit):
    return lax.rem(lax.div(value, 1 << bit), 2)


def flipped(value, mask):
    result = value
    for bit in range(6):
        if mask >> bit & 1:
            result = result + (1 - 2 * bit_of(value, bit)) * (1 << bit)
    return result


def split(value):
    high = value.astype(BF16)
    low = (value - high.astype(F32)).astype(BF16)
    return high, low


def gate_matrix(real, imag):
    rh, rl = split(real)
    ih, il = split(imag)
    top = jnp.concatenate([rh, -ih, rl, -il, rh, -ih], axis=1)
    bottom = jnp.concatenate([ih, rh, il, rl, ih, rh], axis=1)
    return top, bottom


def left(matrix, data):
    high, low = split(data)
    stacked = jnp.concatenate([high, high, low], axis=0)
    return jnp.dot(matrix, stacked, preferred_element_type=F32)


def right(data, matrix):
    high, low = split(data)
    stacked = jnp.concatenate([high, high, low], axis=1)
    return lax.dot_general(
        stacked, matrix, (((1,), (1,)), ((), ())), preferred_element_type=F32
    )


def kernel(
    perm_ref, x_hbm, g_hbm, out_ref, norm_ref,
    x, g, mats, work, rmat, prod,
    s1, a1, t1, s2, a2, t2, u2, stage, recv, f3, g3, k3,
    nsrc, nrecv, qsrc, qrecv,
    load_sem, ssem, rsem, nssem, nrsem, assem, arsem, qssem, qrsem,
):
    hi = lax.axis_index("hi")
    lo = lax.axis_index("lo")
    x_at = lax.div(lo, 2)
    z_at = lax.rem(lo, 2)

    def lo_peer(dx, dz):
        zz = z_at + dz * (1 - 2 * z_at)
        return lax.rem(x_at + dx, 8) * 2 + zz

    def hi_id(mask):
        return (flipped(hi, mask), lo)

    load_x = pltpu.make_async_copy(x_hbm, x, load_sem.at[0])
    load_g0 = pltpu.make_async_copy(g_hbm.at[1], g.at[1], load_sem.at[1])
    load_ga = pltpu.make_async_copy(g_hbm.at[0], g.at[0], load_sem.at[2])
    load_gb = pltpu.make_async_copy(g_hbm.at[pl.ds(2, 14)], g.at[pl.ds(2, 14)], load_sem.at[3])
    load_g0.start()
    load_x.start()
    load_gb.start()
    load_ga.start()

    barrier = pltpu.get_barrier_semaphore()
    hi_masks = NORM_MASKS + [1 << SWAP_BITS[1], 1 << SWAP_BITS[2]]
    for dx, dz in LO_STEPS:
        pl.semaphore_signal(
            barrier, inc=1, device_id=(hi, lo_peer(dx, dz)), device_id_type=MESH
        )
    for mask in hi_masks:
        pl.semaphore_signal(barrier, inc=1, device_id=hi_id(mask), device_id_type=MESH)

    def prepare(slot, gate):
        top, bottom = gate_matrix(g[gate, 0], g[gate, 1])
        mats[slot, 0:128, :] = top
        mats[slot, 128:256, :] = bottom

    def exchange(src, dst, index, mask):
        return pltpu.make_async_remote_copy(
            src_ref=src,
            dst_ref=dst,
            send_sem=ssem.at[index],
            recv_sem=rsem.at[index],
            device_id=hi_id(mask),
            device_id_type=MESH,
        )

    load_g0.wait()
    prepare(0, 1)
    load_x.wait()

    values = x[...].reshape(64, 8, 128)
    nsrc[0] = jnp.sum(jnp.sum(values * values, axis=0), axis=0, keepdims=True)

    data = jnp.concatenate(
        [
            jnp.concatenate([x[pl.ds(c, 128, stride=4), :], x[pl.ds(2 + c, 128, stride=4), :]], axis=1)
            for c in range(2)
        ],
        axis=0,
    )
    y = left(mats[0], data)

    def put_rows(ref, result):
        for c in range(2):
            for b in range(2):
                ref[c, pl.ds(b, 128, stride=2), :] = result[
                    c * 128 : (c + 1) * 128, b * 128 : (b + 1) * 128
                ]

    def get_rows(ref):
        return jnp.concatenate(
            [
                jnp.concatenate(
                    [ref[c, pl.ds(0, 128, stride=2), :], ref[c, pl.ds(1, 128, stride=2), :]], axis=1
                )
                for c in range(2)
            ],
            axis=0,
        )

    put_rows(s1, y)
    pl.semaphore_wait(barrier, len(LO_STEPS) + len(hi_masks))

    def half(side):
        return pl.ds(pl.multiple_of(side * 128, 128), 128)

    side = bit_of(hi, SWAP_BITS[0])
    send1 = exchange(s1.at[:, half(1 - side), :], a1, 0, 1 << SWAP_BITS[0])
    send1.start()
    norm_sends = []
    for i, mask in enumerate(NORM_MASKS):
        copy = pltpu.make_async_remote_copy(
            src_ref=nsrc.at[0],
            dst_ref=nrecv.at[i],
            send_sem=nssem.at[i],
            recv_sem=nrsem.at[i],
            device_id=hi_id(mask),
            device_id_type=MESH,
        )
        copy.start()
        norm_sends.append(copy)

    def gate_mid(slot, read, ref, where):
        result = left(mats[slot], jnp.concatenate([read(0), read(1)], axis=0))
        for c in range(2):
            ref[c, where, :] = result[c * 128 : (c + 1) * 128, :]

    load_gb.wait()
    load_ga.wait()
    prepare(1, 2)
    gate_mid(1, lambda c: s1[c, half(side), :], t1, half(side))
    prepare(2, 5)
    prepare(3, 6)
    prepare(4, 9)
    for b in range(2):
        rows = pl.ds(b, 64, stride=2)
        top, bottom = gate_matrix(g.at[10, 0][rows, :], g.at[10, 1][rows, :])
        mats[5, b * 64 : (b + 1) * 64, :] = top
        mats[5, 128 + b * 64 : 128 + (b + 1) * 64, :] = bottom
    prepare(6, 13)
    prepare(7, 14)

    prod[0:128, :] = g[0, 0]
    prod[128:256, :] = g[0, 1]
    for gate in (3, 4, 7, 8, 11, 12, 15):
        top, bottom = gate_matrix(g[gate, 0], g[gate, 1])
        work[0:128, :] = top
        work[128:256, :] = bottom
        prod[...] = left(work[...], prod[...])
    top, bottom = gate_matrix(prod[0:128, :], prod[128:256, :])
    rmat[0:128, :] = top
    rmat[128:256, :] = bottom

    send1.wait()
    gate_mid(1, lambda c: a1[c], t1, half(1 - side))

    put_rows(s2, left(mats[2], get_rows(t1)))
    side = bit_of(hi, SWAP_BITS[1])
    send2 = exchange(s2.at[:, half(1 - side), :], a2, 1, 1 << SWAP_BITS[1])
    send2.start()
    for copy in norm_sends:
        copy.wait()
    total = nsrc[0]
    for i in range(len(NORM_MASKS)):
        total = total + nrecv[i]
    nsrc[1] = total
    nsend2 = exchange(nsrc.at[1], nrecv.at[15], 4, 1 << SWAP_BITS[1])
    nsend2.start()
    gate_mid(3, lambda c: s2[c, half(side), :], t2, half(side))
    send2.wait()
    gate_mid(3, lambda c: a2[c], t2, half(1 - side))
    nsend2.wait()
    qsrc[0] = nsrc[1] + nrecv[15]

    put_rows(t1, left(mats[4], get_rows(t2)))
    data = jnp.concatenate(
        [jnp.concatenate([t1[c, 0:128, :], t1[c, 128:256, :]], axis=1) for c in range(2)], axis=0
    )
    y = left(mats[5], data)
    for c in range(2):
        for b in range(2):
            for t in range(2):
                base = c * 128 + b * 64
                u2[c, b, t * 8 : (t + 1) * 8] = y[
                    base : base + 64, t * 128 : (t + 1) * 128
                ].reshape(8, 8, 128)

    for j in range(16):
        block = jnp.int32(0)
        for v in range(1, 16):
            block = jnp.where(perm_ref[v] == j, v, block)
        for b in range(2):
            for c in range(2):
                stage[b, j, c] = u2[c, b, block]
    sends = [[], []]
    for b in range(2):
        for dx, dz in LO_STEPS:
            peer = lo_peer(dx, dz)
            copy = pltpu.make_async_remote_copy(
                src_ref=stage.at[b, peer],
                dst_ref=recv.at[b, lo],
                send_sem=assem.at[b, dx * 2 + dz],
                recv_sem=arsem.at[b, dx * 2 + dz],
                device_id=(hi, peer),
                device_id_type=MESH,
            )
            copy.start()
            sends[b].append(copy)
    qsends = []
    for dx, dz in LO_STEPS:
        copy = pltpu.make_async_remote_copy(
            src_ref=qsrc.at[0],
            dst_ref=qrecv.at[dx * 2 + dz],
            send_sem=qssem.at[dx * 2 + dz],
            recv_sem=qrsem.at[dx * 2 + dz],
            device_id=(hi, lo_peer(dx, dz)),
            device_id_type=MESH,
        )
        copy.start()
        qsends.append(copy)
    for b in range(2):
        recv[b, lo] = stage[b, lo]

    side = bit_of(hi, SWAP_BITS[2])

    def quarter(which):
        return pl.ds(pl.multiple_of(which * 64, 64), 64)

    sends3 = []
    for b in range(2):
        for copy in sends[b]:
            copy.wait()
        data = jnp.concatenate(
            [recv[b, :, 0].reshape(128, 128), recv[b, :, 1].reshape(128, 128)], axis=0
        )
        y = left(mats[6], data)
        for c in range(2):
            f3[b, c] = y[c * 128 : (c + 1) * 128, :]
        copy = exchange(f3.at[b, :, quarter(1 - side), :], g3.at[b], 2 + b, 1 << SWAP_BITS[2])
        copy.start()
        sends3.append(copy)
    total = qsrc[0]
    for copy in qsends:
        copy.wait()
    for dx, dz in LO_STEPS:
        total = total + qrecv[dx * 2 + dz]
    qsrc[1] = total
    nsend3 = exchange(qsrc.at[1], qrecv.at[0], 5, 1 << SWAP_BITS[2])
    nsend3.start()

    def finish(where):
        y = left(mats[7], jnp.concatenate([k3[0], k3[1]], axis=0))
        y = right(jnp.concatenate([y[0:128, :], y[128:256, :]], axis=1), rmat[...])
        for c in range(2):
            out_ref[pl.ds(where * 256 + c, 128, stride=2), :] = y[:, c * 128 : (c + 1) * 128]

    for b in range(2):
        for c in range(2):
            k3[c, pl.ds(b, 64, stride=2), :] = f3[b, c, quarter(side), :]
    finish(side)
    for b in range(2):
        sends3[b].wait()
        for c in range(2):
            k3[c, pl.ds(b, 64, stride=2), :] = g3[b, c]
    finish(1 - side)
    nsend3.wait()
    norm_ref[...] = qsrc[1] + qrecv[0]


def per_device(count, state, gates, remap_perm):
    rows = state.reshape(2, 256, 128).transpose(1, 0, 2).reshape(512, 128)
    vm = pltpu.VMEM
    dma = pltpu.SemaphoreType.DMA
    out, norm = pl.pallas_call(
        kernel,
        out_shape=(
            jax.ShapeDtypeStruct((512, 128), F32),
            jax.ShapeDtypeStruct((1, 128), F32),
        ),
        in_specs=[
            pl.BlockSpec(memory_space=pltpu.SMEM),
            pl.BlockSpec(memory_space=pl.ANY),
            pl.BlockSpec(memory_space=pl.ANY),
        ],
        out_specs=(
            pl.BlockSpec(memory_space=pltpu.VMEM),
            pl.BlockSpec(memory_space=pltpu.VMEM),
        ),
        scratch_shapes=[
            vm((512, 128), F32),
            vm((16, 2, 128, 128), F32),
            vm((8, 256, 768), BF16),
            vm((256, 768), BF16),
            vm((256, 768), BF16),
            vm((256, 128), F32),
            vm((2, 256, 128), F32),
            vm((2, 128, 128), F32),
            vm((2, 256, 128), F32),
            vm((2, 256, 128), F32),
            vm((2, 128, 128), F32),
            vm((2, 256, 128), F32),
            vm((2, 2, 16, 8, 128), F32),
            vm((2, 16, 2, 8, 128), F32),
            vm((2, 16, 2, 8, 128), F32),
            vm((2, 2, 128, 128), F32),
            vm((2, 2, 64, 128), F32),
            vm((2, 128, 128), F32),
            vm((2, 1, 128), F32),
            vm((16, 1, 128), F32),
            vm((2, 1, 128), F32),
            vm((16, 1, 128), F32),
            dma((4,)),
            dma((6,)),
            dma((6,)),
            dma((15,)),
            dma((15,)),
            dma((2, 16)),
            dma((2, 16)),
            dma((16,)),
            dma((16,)),
        ],
        compiler_params=pltpu.CompilerParams(collective_id=0, has_side_effects=True),
    )(remap_perm, rows, gates)
    mean_sq = jnp.sum(norm) / count
    scaled = out * (1.0 / jnp.sqrt(mean_sq + 1e-06))
    return scaled.reshape(256, 2, 128).transpose(1, 0, 2).reshape(2, 32768)


def solution(mesh):
    devices = mesh.shape["hi"] * mesh.shape["lo"]
    in_specs = (P(None, ("hi", "lo")), P(), P())
    out_specs = P(None, ("hi", "lo"))
    return jax.shard_map(
        functools.partial(per_device, 2.0 * 32768 * devices),
        mesh=mesh,
        in_specs=in_specs,
        out_specs=out_specs,
        check_vma=False,
    )
```

```python
import functools

import jax
import jax.numpy as jnp
from jax import lax
from jax.experimental import pallas as pl
from jax.experimental.pallas import tpu as pltpu
from jax.sharding import PartitionSpec as P

F32 = jnp.float32
BF16 = jnp.bfloat16
MESH = pl.DeviceIdType.MESH

SWAP_BITS = (4, 0, 3)
NORM_MASKS = [m for m in range(63, 0, -1) if not m >> SWAP_BITS[0] & 1]
Z_MASK = 32
LO_STEPS = sorted(
    [(dx, dz) for dx in range(8) for dz in range(2) if dx or dz],
    key=lambda s: -(min(s[0], 8 - s[0]) + 4 * s[1]),
)


def bit_of(value, bit):
    return lax.rem(lax.div(value, 1 << bit), 2)


def flipped(value, mask):
    result = value
    for bit in range(6):
        if mask >> bit & 1:
            result = result + (1 - 2 * bit_of(value, bit)) * (1 << bit)
    return result


def split(value):
    high = value.astype(BF16)
    low = (value - high.astype(F32)).astype(BF16)
    return high, low


def gate_matrix(real, imag):
    rh, rl = split(real)
    ih, il = split(imag)
    top = jnp.concatenate([rh, -ih, rl, -il, rh, -ih], axis=1)
    bottom = jnp.concatenate([ih, rh, il, rl, ih, rh], axis=1)
    return top, bottom


def left(matrix, data):
    high, low = split(data)
    stacked = jnp.concatenate([high, high, low], axis=0)
    return jnp.dot(matrix, stacked, preferred_element_type=F32)


def right(data, matrix):
    high, low = split(data)
    stacked = jnp.concatenate([high, high, low], axis=1)
    return lax.dot_general(
        stacked, matrix, (((1,), (1,)), ((), ())), preferred_element_type=F32
    )


def kernel(
    count, perm_hbm, x_hbm, g_hbm, out_ref, norm_ref,
    perm_ref, x, g, mats, work, rmat, prod,
    s1, a1, t1, s2, a2, t2, u2, stage, recv, f3, g3, k3,
    nsrc, nrecv, qsrc, qrecv,
    wave, ready, load_sem, ssem, rsem, nssem, nrsem, assem, arsem, qssem, qrsem,
):
    hi = lax.axis_index("hi")
    lo = lax.axis_index("lo")
    x_at = lax.div(lo, 2)
    z_at = lax.rem(lo, 2)

    def lo_peer(dx, dz):
        zz = z_at + dz * (1 - 2 * z_at)
        return lax.rem(x_at + dx, 8) * 2 + zz

    def hi_id(mask):
        return (flipped(hi, mask), lo)

    load_x = pltpu.make_async_copy(x_hbm, x, load_sem.at[0])
    load_g0 = pltpu.make_async_copy(g_hbm.at[1], g.at[1], load_sem.at[1])
    load_ga = pltpu.make_async_copy(g_hbm.at[0], g.at[0], load_sem.at[2])
    load_gb = pltpu.make_async_copy(g_hbm.at[pl.ds(2, 14)], g.at[pl.ds(2, 14)], load_sem.at[3])
    load_perm = pltpu.make_async_copy(perm_hbm, perm_ref, load_sem.at[4])
    load_g0.start()
    load_x.start()

    z_bit = bit_of(hi, 5)
    y_at = lax.rem(lax.div(hi, 2), 8)

    def y_id(step):
        return (hi + 2 * (lax.rem(y_at + step, 8) - y_at), lo)

    around = [(hi, lo_peer(1, 0)), (hi, lo_peer(7, 0)), y_id(1), y_id(7)]
    barrier = pltpu.get_barrier_semaphore()

    def signal(sem, peer):
        pl.semaphore_signal(sem, inc=1, device_id=peer, device_id_type=MESH)

    signal(barrier, hi_id(1 << SWAP_BITS[0]))
    for peer in around:
        signal(barrier, peer)
    signal(barrier, hi_id(1 << SWAP_BITS[1]))

    @pl.when(z_at == 0)
    def _():
        signal(barrier, (hi, lo_peer(0, 1)))

    @pl.when(z_bit == 0)
    def _():
        signal(barrier, hi_id(Z_MASK))

    load_gb.start()
    load_ga.start()
    load_perm.start()

    def tell():
        for i, peer in enumerate(around):
            signal(wave.at[i], peer)

    def hear():
        for i in range(4):
            pl.semaphore_wait(wave.at[i], 1)

    def prepare(slot, gate):
        top, bottom = gate_matrix(g[gate, 0], g[gate, 1])
        mats[slot, 0:128, :] = top
        mats[slot, 128:256, :] = bottom

    def exchange(src, dst, index, mask):
        return pltpu.make_async_remote_copy(
            src_ref=src,
            dst_ref=dst,
            send_sem=ssem.at[index],
            recv_sem=rsem.at[index],
            device_id=hi_id(mask),
            device_id_type=MESH,
        )

    load_g0.wait()
    prepare(0, 1)
    load_x.wait()

    values = x[...].reshape(64, 8, 128)
    nsrc[0] = jnp.sum(jnp.sum(values * values, axis=0), axis=0, keepdims=True)

    data = jnp.concatenate(
        [
            jnp.concatenate([x[pl.ds(c, 128, stride=4), :], x[pl.ds(2 + c, 128, stride=4), :]], axis=1)
            for c in range(2)
        ],
        axis=0,
    )
    y = left(mats[0], data)

    def put_rows(ref, result):
        for c in range(2):
            for b in range(2):
                ref[c, pl.ds(b, 128, stride=2), :] = result[
                    c * 128 : (c + 1) * 128, b * 128 : (b + 1) * 128
                ]

    def get_rows(ref):
        return jnp.concatenate(
            [
                jnp.concatenate(
                    [ref[c, pl.ds(0, 128, stride=2), :], ref[c, pl.ds(1, 128, stride=2), :]], axis=1
                )
                for c in range(2)
            ],
            axis=0,
        )

    put_rows(s1, y)
    pl.semaphore_wait(barrier, 6 + z_at + z_bit)

    def half(side):
        return pl.ds(pl.multiple_of(side * 128, 128), 128)

    side = bit_of(hi, SWAP_BITS[0])
    send1 = exchange(s1.at[:, half(1 - side), :], a1, 0, 1 << SWAP_BITS[0])
    send1.start()
    nsend1 = exchange(nsrc.at[0], nrecv.at[0], 4, 1 << SWAP_BITS[0])
    nsend1.start()
    tell()

    def gate_mid(slot, read, ref, where):
        result = left(mats[slot], jnp.concatenate([read(0), read(1)], axis=0))
        for c in range(2):
            ref[c, where, :] = result[c * 128 : (c + 1) * 128, :]

    load_gb.wait()
    prepare(1, 2)
    hear()
    tell()
    gate_mid(1, lambda c: s1[c, half(side), :], t1, half(side))
    hear()
    tell()
    prepare(2, 5)
    prepare(3, 6)
    prepare(4, 9)
    hear()
    tell()
    for b in range(2):
        rows = pl.ds(b, 64, stride=2)
        top, bottom = gate_matrix(g.at[10, 0][rows, :], g.at[10, 1][rows, :])
        mats[5, b * 64 : (b + 1) * 64, :] = top
        mats[5, 128 + b * 64 : 128 + (b + 1) * 64, :] = bottom
    hear()

    @pl.when(z_at == 1)
    def _():
        signal(ready.at[0], (hi, lo_peer(0, 1)))

    @pl.when(z_bit == 1)
    def _():
        signal(ready.at[1], hi_id(Z_MASK))

    nsend1.wait()
    qsrc[0] = nsrc[0] + nrecv[0]
    qsends = []
    for dx, dz in LO_STEPS:
        qsends.append(
            pltpu.make_async_remote_copy(
                src_ref=qsrc.at[0],
                dst_ref=qrecv.at[dx * 2 + dz],
                send_sem=qssem.at[dx * 2 + dz],
                recv_sem=qrsem.at[dx * 2 + dz],
                device_id=(hi, lo_peer(dx, dz)),
                device_id_type=MESH,
            )
        )

    @pl.when(z_at == 1)
    def _():
        for copy in qsends:
            copy.start()

    send1.wait()
    gate_mid(1, lambda c: a1[c], t1, half(1 - side))

    put_rows(s2, left(mats[2], get_rows(t1)))
    side = bit_of(hi, SWAP_BITS[1])
    send2 = exchange(s2.at[:, half(1 - side), :], a2, 1, 1 << SWAP_BITS[1])
    send2.start()
    gate_mid(3, lambda c: s2[c, half(side), :], t2, half(side))
    send2.wait()
    gate_mid(3, lambda c: a2[c], t2, half(1 - side))

    put_rows(t1, left(mats[4], get_rows(t2)))
    data = jnp.concatenate(
        [jnp.concatenate([t1[c, 0:128, :], t1[c, 128:256, :]], axis=1) for c in range(2)], axis=0
    )
    y = left(mats[5], data)
    for c in range(2):
        for b in range(2):
            for t in range(2):
                base = c * 128 + b * 64
                u2[c, b, t * 8 : (t + 1) * 8] = y[
                    base : base + 64, t * 128 : (t + 1) * 128
                ].reshape(8, 8, 128)

    load_perm.wait()
    for j in range(16):
        block = jnp.int32(0)
        for v in range(1, 16):
            block = jnp.where(perm_ref[v] == j, v, block)
        for b in range(2):
            for c in range(2):
                stage[b, j, c] = u2[c, b, block]
    @pl.when(z_at == 0)
    def _():
        pl.semaphore_wait(ready.at[0], 1)
        for copy in qsends:
            copy.start()

    sends = [[], []]
    for b in range(2):
        for dx, dz in LO_STEPS:
            peer = lo_peer(dx, dz)
            copy = pltpu.make_async_remote_copy(
                src_ref=stage.at[b, peer],
                dst_ref=recv.at[b, lo],
                send_sem=assem.at[b, dx * 2 + dz],
                recv_sem=arsem.at[b, dx * 2 + dz],
                device_id=(hi, peer),
                device_id_type=MESH,
            )
            copy.start()
            sends[b].append(copy)
    for b in range(2):
        recv[b, lo] = stage[b, lo]

    load_ga.wait()
    prepare(6, 13)
    prepare(7, 14)
    prod[0:128, :] = g[0, 0]
    prod[128:256, :] = g[0, 1]
    for gate in (3, 4, 7, 8, 11, 12, 15):
        top, bottom = gate_matrix(g[gate, 0], g[gate, 1])
        work[0:128, :] = top
        work[128:256, :] = bottom
        prod[...] = left(work[...], prod[...])
    top, bottom = gate_matrix(prod[0:128, :], prod[128:256, :])
    rmat[0:128, :] = top
    rmat[128:256, :] = bottom


    total = qsrc[0]
    for copy in qsends:
        copy.wait()
    for dx, dz in LO_STEPS:
        total = total + qrecv[dx * 2 + dz]
    qsrc[1] = total

    @pl.when(z_bit == 0)
    def _():
        pl.semaphore_wait(ready.at[1], 1)

    norm_sends = []
    for i, mask in enumerate(NORM_MASKS):
        copy = pltpu.make_async_remote_copy(
            src_ref=qsrc.at[1],
            dst_ref=nrecv.at[1 + i],
            send_sem=nssem.at[i],
            recv_sem=nrsem.at[i],
            device_id=hi_id(mask),
            device_id_type=MESH,
        )
        copy.start()
        norm_sends.append(copy)

    side = bit_of(hi, SWAP_BITS[2])

    def quarter(which):
        return pl.ds(pl.multiple_of(which * 64, 64), 64)

    sends3 = []
    for b in range(2):
        for copy in sends[b]:
            copy.wait()
        data = jnp.concatenate(
            [recv[b, :, 0].reshape(128, 128), recv[b, :, 1].reshape(128, 128)], axis=0
        )
        y = left(mats[6], data)
        for c in range(2):
            f3[b, c] = y[c * 128 : (c + 1) * 128, :]
        copy = exchange(f3.at[b, :, quarter(1 - side), :], g3.at[b], 2 + b, 1 << SWAP_BITS[2])
        copy.start()
        sends3.append(copy)
    def finish(where):
        y = left(mats[7], jnp.concatenate([k3[0], k3[1]], axis=0))
        y = right(jnp.concatenate([y[0:128, :], y[128:256, :]], axis=1), rmat[...])
        for c in range(2):
            out_ref[pl.ds(where * 256 + c, 128, stride=2), :] = y[:, c * 128 : (c + 1) * 128]

    for b in range(2):
        for c in range(2):
            k3[c, pl.ds(b, 64, stride=2), :] = f3[b, c, quarter(side), :]
    finish(side)
    for b in range(2):
        sends3[b].wait()
        for c in range(2):
            k3[c, pl.ds(b, 64, stride=2), :] = g3[b, c]
    finish(1 - side)
    total = qsrc[1]
    for copy in norm_sends:
        copy.wait()
    for i in range(len(NORM_MASKS)):
        total = total + nrecv[1 + i]
    mean_sq = jnp.sum(total, axis=1, keepdims=True) / count
    norm_ref[...] = jnp.broadcast_to(1.0 / jnp.sqrt(mean_sq + 1e-06), (1, 128))


def per_device(count, state, gates, remap_perm):
    rows = state.reshape(2, 256, 128).transpose(1, 0, 2).reshape(512, 128)
    vm = pltpu.VMEM
    dma = pltpu.SemaphoreType.DMA
    out, norm = pl.pallas_call(
        functools.partial(kernel, count),
        out_shape=(vm((512, 128), F32), vm((1, 128), F32)),
        in_specs=[
            pl.BlockSpec(memory_space=pl.ANY),
            pl.BlockSpec(memory_space=pl.ANY),
            pl.BlockSpec(memory_space=pl.ANY),
        ],
        out_specs=(
            pl.BlockSpec(memory_space=pltpu.VMEM),
            pl.BlockSpec(memory_space=pltpu.VMEM),
        ),
        scratch_shapes=[
            pltpu.SMEM((16,), jnp.int32),
            vm((512, 128), F32),
            vm((16, 2, 128, 128), F32),
            vm((8, 256, 768), BF16),
            vm((256, 768), BF16),
            vm((256, 768), BF16),
            vm((256, 128), F32),
            vm((2, 256, 128), F32),
            vm((2, 128, 128), F32),
            vm((2, 256, 128), F32),
            vm((2, 256, 128), F32),
            vm((2, 128, 128), F32),
            vm((2, 256, 128), F32),
            vm((2, 2, 16, 8, 128), F32),
            vm((2, 16, 2, 8, 128), F32),
            vm((2, 16, 2, 8, 128), F32),
            vm((2, 2, 128, 128), F32),
            vm((2, 2, 64, 128), F32),
            vm((2, 128, 128), F32),
            vm((1, 1, 128), F32),
            vm((32, 1, 128), F32),
            vm((2, 1, 128), F32),
            vm((16, 1, 128), F32),
            pltpu.SemaphoreType.REGULAR((4,)),
            pltpu.SemaphoreType.REGULAR((2,)),
            dma((5,)),
            dma((5,)),
            dma((5,)),
            dma((31,)),
            dma((31,)),
            dma((2, 16)),
            dma((2, 16)),
            dma((16,)),
            dma((16,)),
        ],
        compiler_params=pltpu.CompilerParams(collective_id=0, has_side_effects=True),
    )(remap_perm, rows, gates)
    return (out * norm).reshape(256, 2, 128).transpose(1, 0, 2).reshape(2, 32768)


def solution(mesh):
    devices = mesh.shape["hi"] * mesh.shape["lo"]
    in_specs = (P(None, ("hi", "lo")), P(), P())
    out_specs = P(None, ("hi", "lo"))
    return jax.shard_map(
        functools.partial(per_device, 2.0 * 32768 * devices),
        mesh=mesh,
        in_specs=in_specs,
        out_specs=out_specs,
        check_vma=False,
    )
```

```python
import functools

import jax
import jax.numpy as jnp
from jax import lax
from jax.experimental import pallas as pl
from jax.experimental.pallas import tpu as pltpu
from jax.sharding import PartitionSpec as P

F32 = jnp.float32
BF16 = jnp.bfloat16
MESH = pl.DeviceIdType.MESH

SWAP_BITS = (4, 0, 3)
NORM_MASKS = [m for m in range(63, 0, -1) if not m >> SWAP_BITS[0] & 1]
Z_MASK = 32
LO_STEPS = sorted(
    [(dx, dz) for dx in range(8) for dz in range(2) if dx or dz],
    key=lambda s: -(min(s[0], 8 - s[0]) + 4 * s[1]),
)


def bit_of(value, bit):
    return lax.rem(lax.div(value, 1 << bit), 2)


def flipped(value, mask):
    result = value
    for bit in range(6):
        if mask >> bit & 1:
            result = result + (1 - 2 * bit_of(value, bit)) * (1 << bit)
    return result


def split(value):
    high = value.astype(BF16)
    low = (value - high.astype(F32)).astype(BF16)
    return high, low


def gate_matrix(real, imag):
    rh, rl = split(real)
    ih, il = split(imag)
    top = jnp.concatenate([rh, -ih, rl, -il, rh, -ih], axis=1)
    bottom = jnp.concatenate([ih, rh, il, rl, ih, rh], axis=1)
    return top, bottom


def left(matrix, data):
    high, low = split(data)
    stacked = jnp.concatenate([high, high, low], axis=0)
    return jnp.dot(matrix, stacked, preferred_element_type=F32)


def right(data, matrix):
    high, low = split(data)
    stacked = jnp.concatenate([high, high, low], axis=1)
    return lax.dot_general(
        stacked, matrix, (((1,), (1,)), ((), ())), preferred_element_type=F32
    )


def kernel(
    count, perm_hbm, x_hbm, g_hbm, out_ref, norm_ref,
    perm_ref, x, g, mats, work, rmat, prod,
    s1, a1, t1, s2, a2, t2, u2, stage, recv, f3, g3, k3,
    nsrc, nrecv, qsrc, qrecv,
    wave, ready, load_sem, ssem, rsem, nssem, nrsem, assem, arsem, qssem, qrsem,
):
    hi = lax.axis_index("hi")
    lo = lax.axis_index("lo")
    x_at = lax.div(lo, 2)
    z_at = lax.rem(lo, 2)

    def lo_peer(dx, dz):
        zz = z_at + dz * (1 - 2 * z_at)
        return lax.rem(x_at + dx, 8) * 2 + zz

    def hi_id(mask):
        return (flipped(hi, mask), lo)

    load_x = pltpu.make_async_copy(x_hbm, x, load_sem.at[0])
    load_g0 = pltpu.make_async_copy(g_hbm.at[1], g.at[1], load_sem.at[1])
    load_ga = pltpu.make_async_copy(g_hbm.at[0], g.at[0], load_sem.at[2])
    load_gb = pltpu.make_async_copy(g_hbm.at[pl.ds(2, 14)], g.at[pl.ds(2, 14)], load_sem.at[3])
    load_perm = pltpu.make_async_copy(perm_hbm, perm_ref, load_sem.at[4])
    load_g0.start()
    load_x.start()

    z_bit = bit_of(hi, 5)
    y_at = lax.rem(lax.div(hi, 2), 8)

    def y_id(step):
        return (hi + 2 * (lax.rem(y_at + step, 8) - y_at), lo)

    around = [(hi, lo_peer(2, 0)), (hi, lo_peer(6, 0)), y_id(2), y_id(6)]
    near = [(hi, lo_peer(1, 0)), (hi, lo_peer(7, 0)), y_id(1), y_id(7)]
    barrier = pltpu.get_barrier_semaphore()

    def signal(sem, peer):
        pl.semaphore_signal(sem, inc=1, device_id=peer, device_id_type=MESH)

    signal(barrier, hi_id(1 << SWAP_BITS[0]))
    for peer in around + near:
        signal(barrier, peer)
    signal(barrier, hi_id(1 << SWAP_BITS[1]))

    @pl.when(z_at == 0)
    def _():
        for dx in range(8):
            signal(barrier, (hi, lo_peer(dx, 1)))

    @pl.when(z_bit == 0)
    def _():
        for y_mask in range(0, 16, 2):
            signal(barrier, hi_id(Z_MASK | y_mask))

    load_gb.start()
    load_ga.start()
    load_perm.start()

    def tell():
        for i, peer in enumerate(around):
            signal(wave.at[i], peer)

    def hear():
        for i in range(4):
            pl.semaphore_wait(wave.at[i], 1)

    def prepare(slot, gate):
        top, bottom = gate_matrix(g[gate, 0], g[gate, 1])
        mats[slot, 0:128, :] = top
        mats[slot, 128:256, :] = bottom

    def exchange(src, dst, index, mask):
        return pltpu.make_async_remote_copy(
            src_ref=src,
            dst_ref=dst,
            send_sem=ssem.at[index],
            recv_sem=rsem.at[index],
            device_id=hi_id(mask),
            device_id_type=MESH,
        )

    load_g0.wait()
    prepare(0, 1)
    load_x.wait()

    data = jnp.concatenate(
        [
            jnp.concatenate([x[pl.ds(c, 128, stride=4), :], x[pl.ds(2 + c, 128, stride=4), :]], axis=1)
            for c in range(2)
        ],
        axis=0,
    )
    y = left(mats[0], data)

    def put_rows(ref, result):
        for c in range(2):
            for b in range(2):
                ref[c, pl.ds(b, 128, stride=2), :] = result[
                    c * 128 : (c + 1) * 128, b * 128 : (b + 1) * 128
                ]

    def get_rows(ref):
        return jnp.concatenate(
            [
                jnp.concatenate(
                    [ref[c, pl.ds(0, 128, stride=2), :], ref[c, pl.ds(1, 128, stride=2), :]], axis=1
                )
                for c in range(2)
            ],
            axis=0,
        )

    put_rows(s1, y)
    pl.semaphore_wait(barrier, 10 + 8 * z_at + 8 * z_bit)

    def half(side):
        return pl.ds(pl.multiple_of(side * 128, 128), 128)

    side = bit_of(hi, SWAP_BITS[0])
    send1 = exchange(s1.at[:, half(1 - side), :], a1, 0, 1 << SWAP_BITS[0])
    send1.start()

    values = x[...].reshape(64, 8, 128)
    nsrc[0] = jnp.sum(jnp.sum(values * values, axis=0), axis=0, keepdims=True)
    nsend1 = exchange(nsrc.at[0], nrecv.at[0], 4, 1 << SWAP_BITS[0])
    nsend1.start()
    tell()

    def gate_mid(slot, read, ref, where):
        result = left(mats[slot], jnp.concatenate([read(0), read(1)], axis=0))
        for c in range(2):
            ref[c, where, :] = result[c * 128 : (c + 1) * 128, :]

    load_gb.wait()
    prepare(1, 2)
    gate_mid(1, lambda c: s1[c, half(side), :], t1, half(side))
    prepare(2, 5)
    prepare(3, 6)
    prepare(4, 9)
    for b in range(2):
        rows = pl.ds(b, 64, stride=2)
        top, bottom = gate_matrix(g.at[10, 0][rows, :], g.at[10, 1][rows, :])
        mats[5, b * 64 : (b + 1) * 64, :] = top
        mats[5, 128 + b * 64 : 128 + (b + 1) * 64, :] = bottom
    nsend1.wait()
    qsrc[0] = nsrc[0] + nrecv[0]
    qsends = []
    for dx, dz in LO_STEPS:
        qsends.append(
            pltpu.make_async_remote_copy(
                src_ref=qsrc.at[0],
                dst_ref=qrecv.at[dx * 2 + dz],
                send_sem=qssem.at[dx * 2 + dz],
                recv_sem=qrsem.at[dx * 2 + dz],
                device_id=(hi, lo_peer(dx, dz)),
                device_id_type=MESH,
            )
        )

    send1.wait()
    gate_mid(1, lambda c: a1[c], t1, half(1 - side))

    put_rows(s2, left(mats[2], get_rows(t1)))
    side = bit_of(hi, SWAP_BITS[1])
    send2 = exchange(s2.at[:, half(1 - side), :], a2, 1, 1 << SWAP_BITS[1])
    send2.start()

    hear()
    signal(ready.at[2], hi_id(1 << SWAP_BITS[1]))

    @pl.when(z_at == 1)
    def _():
        signal(ready.at[0], (hi, lo_peer(0, 1)))

    @pl.when(z_at == 1)
    def _():
        for copy in qsends:
            copy.start()

    gate_mid(3, lambda c: s2[c, half(side), :], t2, half(side))
    send2.wait()

    gate_mid(3, lambda c: a2[c], t2, half(1 - side))

    put_rows(t1, left(mats[4], get_rows(t2)))
    data = jnp.concatenate(
        [jnp.concatenate([t1[c, 0:128, :], t1[c, 128:256, :]], axis=1) for c in range(2)], axis=0
    )
    y = left(mats[5], data)
    for c in range(2):
        for b in range(2):
            for t in range(2):
                base = c * 128 + b * 64
                u2[c, b, t * 8 : (t + 1) * 8] = y[
                    base : base + 64, t * 128 : (t + 1) * 128
                ].reshape(8, 8, 128)

    load_perm.wait()
    for j in range(16):
        block = jnp.int32(0)
        for v in range(1, 16):
            block = jnp.where(perm_ref[v] == j, v, block)
        for b in range(2):
            for c in range(2):
                stage[b, j, c] = u2[c, b, block]
    sends = {}
    for b in range(2):
        for dx, dz in LO_STEPS:
            peer = lo_peer(dx, dz)
            sends[b, dx, dz] = pltpu.make_async_remote_copy(
                src_ref=stage.at[b, peer],
                dst_ref=recv.at[b, lo],
                send_sem=assem.at[b, dx * 2 + dz],
                recv_sem=arsem.at[b, dx * 2 + dz],
                device_id=(hi, peer),
                device_id_type=MESH,
            )

    def start(across):
        for b in range(2):
            for dx, dz in LO_STEPS:
                if dz == across:
                    sends[b, dx, dz].start()

    @pl.when(z_at == 0)
    def _():
        start(0)
        pl.semaphore_wait(ready.at[0], 1)
        for copy in qsends:
            copy.start()
        start(1)

    @pl.when(z_at == 1)
    def _():
        start(1)
        start(0)

    for b in range(2):
        recv[b, lo] = stage[b, lo]

    pl.semaphore_wait(ready.at[2], 1)

    @pl.when(z_bit == 1)
    def _():
        signal(ready.at[1], hi_id(Z_MASK))

    load_ga.wait()
    prepare(6, 13)
    prepare(7, 14)
    prod[0:128, :] = g[0, 0]
    prod[128:256, :] = g[0, 1]
    for gate in (3, 4, 7, 8, 11, 12, 15):
        top, bottom = gate_matrix(g[gate, 0], g[gate, 1])
        work[0:128, :] = top
        work[128:256, :] = bottom
        prod[...] = left(work[...], prod[...])
    top, bottom = gate_matrix(prod[0:128, :], prod[128:256, :])
    rmat[0:128, :] = top
    rmat[128:256, :] = bottom


    total = qsrc[0]
    for copy in qsends:
        copy.wait()
    for dx, dz in LO_STEPS:
        total = total + qrecv[dx * 2 + dz]
    qsrc[1] = total

    @pl.when(z_bit == 0)
    def _():
        pl.semaphore_wait(ready.at[1], 1)

    norm_sends = []
    for i, mask in enumerate(NORM_MASKS):
        copy = pltpu.make_async_remote_copy(
            src_ref=qsrc.at[1],
            dst_ref=nrecv.at[1 + i],
            send_sem=nssem.at[i],
            recv_sem=nrsem.at[i],
            device_id=hi_id(mask),
            device_id_type=MESH,
        )
        copy.start()
        norm_sends.append(copy)

    side = bit_of(hi, SWAP_BITS[2])

    def quarter(which):
        return pl.ds(pl.multiple_of(which * 64, 64), 64)

    sends3 = []
    for b in range(2):
        for dx, dz in LO_STEPS:
            sends[b, dx, dz].wait()
        data = jnp.concatenate(
            [recv[b, :, 0].reshape(128, 128), recv[b, :, 1].reshape(128, 128)], axis=0
        )
        y = left(mats[6], data)
        for c in range(2):
            f3[b, c] = y[c * 128 : (c + 1) * 128, :]
        copy = exchange(f3.at[b, :, quarter(1 - side), :], g3.at[b], 2 + b, 1 << SWAP_BITS[2])
        copy.start()
        sends3.append(copy)
    def finish(where):
        y = left(mats[7], jnp.concatenate([k3[0], k3[1]], axis=0))
        y = right(jnp.concatenate([y[0:128, :], y[128:256, :]], axis=1), rmat[...])
        for c in range(2):
            out_ref[pl.ds(where * 256 + c, 128, stride=2), :] = y[:, c * 128 : (c + 1) * 128]

    for b in range(2):
        for c in range(2):
            k3[c, pl.ds(b, 64, stride=2), :] = f3[b, c, quarter(side), :]
    finish(side)
    for b in range(2):
        sends3[b].wait()
        for c in range(2):
            k3[c, pl.ds(b, 64, stride=2), :] = g3[b, c]
    finish(1 - side)
    total = qsrc[1]
    for copy in norm_sends:
        copy.wait()
    for i in range(len(NORM_MASKS)):
        total = total + nrecv[1 + i]
    mean_sq = jnp.sum(total, axis=1, keepdims=True) / count
    norm_ref[...] = jnp.broadcast_to(1.0 / jnp.sqrt(mean_sq + 1e-06), (1, 128))


def per_device(count, state, gates, remap_perm):
    rows = state.reshape(2, 256, 128).transpose(1, 0, 2).reshape(512, 128)
    vm = pltpu.VMEM
    dma = pltpu.SemaphoreType.DMA
    out, norm = pl.pallas_call(
        functools.partial(kernel, count),
        out_shape=(vm((512, 128), F32), vm((1, 128), F32)),
        in_specs=[
            pl.BlockSpec(memory_space=pl.ANY),
            pl.BlockSpec(memory_space=pl.ANY),
            pl.BlockSpec(memory_space=pl.ANY),
        ],
        out_specs=(
            pl.BlockSpec(memory_space=pltpu.VMEM),
            pl.BlockSpec(memory_space=pltpu.VMEM),
        ),
        scratch_shapes=[
            pltpu.SMEM((16,), jnp.int32),
            vm((512, 128), F32),
            vm((16, 2, 128, 128), F32),
            vm((8, 256, 768), BF16),
            vm((256, 768), BF16),
            vm((256, 768), BF16),
            vm((256, 128), F32),
            vm((2, 256, 128), F32),
            vm((2, 128, 128), F32),
            vm((2, 256, 128), F32),
            vm((2, 256, 128), F32),
            vm((2, 128, 128), F32),
            vm((2, 256, 128), F32),
            vm((2, 2, 16, 8, 128), F32),
            vm((2, 16, 2, 8, 128), F32),
            vm((2, 16, 2, 8, 128), F32),
            vm((2, 2, 128, 128), F32),
            vm((2, 2, 64, 128), F32),
            vm((2, 128, 128), F32),
            vm((1, 1, 128), F32),
            vm((32, 1, 128), F32),
            vm((2, 1, 128), F32),
            vm((16, 1, 128), F32),
            pltpu.SemaphoreType.REGULAR((4,)),
            pltpu.SemaphoreType.REGULAR((3,)),
            dma((5,)),
            dma((5,)),
            dma((5,)),
            dma((31,)),
            dma((31,)),
            dma((2, 16)),
            dma((2, 16)),
            dma((16,)),
            dma((16,)),
        ],
        compiler_params=pltpu.CompilerParams(collective_id=0, has_side_effects=True),
    )(remap_perm, rows, gates)
    return (out * norm).reshape(256, 2, 128).transpose(1, 0, 2).reshape(2, 32768)


def solution(mesh):
    devices = mesh.shape["hi"] * mesh.shape["lo"]
    in_specs = (P(None, ("hi", "lo")), P(), P())
    out_specs = P(None, ("hi", "lo"))
    return jax.shard_map(
        functools.partial(per_device, 2.0 * 32768 * devices),
        mesh=mesh,
        in_specs=in_specs,
        out_specs=out_specs,
        check_vma=False,
    )
```

```python
import functools

import jax
import jax.numpy as jnp
from jax import lax
from jax.experimental import pallas as pl
from jax.experimental.pallas import tpu as pltpu
from jax.sharding import PartitionSpec as P

F32 = jnp.float32
BF16 = jnp.bfloat16
MESH = pl.DeviceIdType.MESH

SWAP_BITS = (4, 0, 3)
NORM_MASKS = [m for m in range(63, 0, -1) if not m >> SWAP_BITS[0] & 1]
Z_MASK = 32
LO_STEPS = sorted(
    [(dx, dz) for dx in range(8) for dz in range(2) if dx or dz],
    key=lambda s: -(min(s[0], 8 - s[0]) + 4 * s[1]),
)


def bit_of(value, bit):
    return lax.rem(lax.div(value, 1 << bit), 2)


def flipped(value, mask):
    result = value
    for bit in range(6):
        if mask >> bit & 1:
            result = result + (1 - 2 * bit_of(value, bit)) * (1 << bit)
    return result


def split(value):
    high = value.astype(BF16)
    low = (value - high.astype(F32)).astype(BF16)
    return high, low


def gate_matrix(real, imag):
    rh, rl = split(real)
    ih, il = split(imag)
    top = jnp.concatenate([rh, -ih, rl, -il, rh, -ih], axis=1)
    bottom = jnp.concatenate([ih, rh, il, rl, ih, rh], axis=1)
    return top, bottom


def left(matrix, data):
    high, low = split(data)
    stacked = jnp.concatenate([high, high, low], axis=0)
    return jnp.dot(matrix, stacked, preferred_element_type=F32)


def right(data, matrix):
    high, low = split(data)
    stacked = jnp.concatenate([high, high, low], axis=1)
    return lax.dot_general(
        stacked, matrix, (((1,), (1,)), ((), ())), preferred_element_type=F32
    )


def kernel(
    count, perm_hbm, x_hbm, g_hbm, out_ref, norm_ref,
    perm_ref, x, g, mats, work, rmat, prod,
    s1, a1, t1, s2, a2, t2, u2, stage, recv, f3, g3, k3,
    nsrc, nrecv, qsrc, qrecv,
    wave, ready, load_sem, ssem, rsem, nssem, nrsem, assem, arsem, qssem, qrsem,
):
    hi = lax.axis_index("hi")
    lo = lax.axis_index("lo")
    x_at = lax.div(lo, 2)
    z_at = lax.rem(lo, 2)

    def lo_peer(dx, dz):
        zz = z_at + dz * (1 - 2 * z_at)
        return lax.rem(x_at + dx, 8) * 2 + zz

    def hi_id(mask):
        return (flipped(hi, mask), lo)

    load_x = pltpu.make_async_copy(x_hbm, x, load_sem.at[0])
    load_g0 = pltpu.make_async_copy(g_hbm.at[1], g.at[1], load_sem.at[1])
    load_ga = pltpu.make_async_copy(g_hbm.at[0], g.at[0], load_sem.at[2])
    load_gb = pltpu.make_async_copy(g_hbm.at[pl.ds(2, 14)], g.at[pl.ds(2, 14)], load_sem.at[3])
    load_perm = pltpu.make_async_copy(perm_hbm, perm_ref, load_sem.at[4])
    load_g0.start()
    load_x.start()
    load_perm.start()
    load_gb.start()
    load_ga.start()

    z_bit = bit_of(hi, 5)
    y_at = lax.rem(lax.div(hi, 2), 8)

    def y_id(step):
        return (hi + 2 * (lax.rem(y_at + step, 8) - y_at), lo)

    around = [(hi, lo_peer(2, 0)), (hi, lo_peer(6, 0)), y_id(2), y_id(6)]
    near = [(hi, lo_peer(1, 0)), (hi, lo_peer(7, 0)), y_id(1), y_id(7)]
    barrier = pltpu.get_barrier_semaphore()

    def signal(sem, peer):
        pl.semaphore_signal(sem, inc=1, device_id=peer, device_id_type=MESH)

    signal(barrier, hi_id(1 << SWAP_BITS[0]))
    for peer in around + near:
        signal(barrier, peer)
    signal(barrier, hi_id(1 << SWAP_BITS[1]))

    @pl.when(z_at == 0)
    def _():
        for dx in range(8):
            signal(barrier, (hi, lo_peer(dx, 1)))

    @pl.when(z_bit == 0)
    def _():
        for y_mask in range(0, 16, 2):
            signal(barrier, hi_id(Z_MASK | y_mask))

    def tell():
        for i, peer in enumerate(around):
            signal(wave.at[i], peer)

    def hear():
        for i in range(4):
            pl.semaphore_wait(wave.at[i], 1)

    def prepare(slot, gate):
        top, bottom = gate_matrix(g[gate, 0], g[gate, 1])
        mats[slot, 0:128, :] = top
        mats[slot, 128:256, :] = bottom

    def exchange(src, dst, index, mask):
        return pltpu.make_async_remote_copy(
            src_ref=src,
            dst_ref=dst,
            send_sem=ssem.at[index],
            recv_sem=rsem.at[index],
            device_id=hi_id(mask),
            device_id_type=MESH,
        )

    load_g0.wait()
    prepare(0, 1)
    load_x.wait()

    data = jnp.concatenate(
        [
            jnp.concatenate([x[pl.ds(c, 128, stride=4), :], x[pl.ds(2 + c, 128, stride=4), :]], axis=1)
            for c in range(2)
        ],
        axis=0,
    )
    y = left(mats[0], data)

    def put_rows(ref, result):
        for c in range(2):
            for b in range(2):
                ref[c, pl.ds(b, 128, stride=2), :] = result[
                    c * 128 : (c + 1) * 128, b * 128 : (b + 1) * 128
                ]

    def get_rows(ref):
        return jnp.concatenate(
            [
                jnp.concatenate(
                    [ref[c, pl.ds(0, 128, stride=2), :], ref[c, pl.ds(1, 128, stride=2), :]], axis=1
                )
                for c in range(2)
            ],
            axis=0,
        )

    put_rows(s1, y)
    pl.semaphore_wait(barrier, 10 + 8 * z_at + 8 * z_bit)

    def half(side):
        return pl.ds(pl.multiple_of(side * 128, 128), 128)

    side = bit_of(hi, SWAP_BITS[0])
    send1 = exchange(s1.at[:, half(1 - side), :], a1, 0, 1 << SWAP_BITS[0])
    send1.start()

    values = x[...].reshape(64, 8, 128)
    nsrc[0] = jnp.sum(jnp.sum(values * values, axis=0), axis=0, keepdims=True)
    nsend1 = exchange(nsrc.at[0], nrecv.at[0], 4, 1 << SWAP_BITS[0])
    nsend1.start()
    tell()

    def gate_mid(slot, read, ref, where):
        result = left(mats[slot], jnp.concatenate([read(0), read(1)], axis=0))
        for c in range(2):
            ref[c, where, :] = result[c * 128 : (c + 1) * 128, :]

    load_gb.wait()
    prepare(1, 2)
    gate_mid(1, lambda c: s1[c, half(side), :], t1, half(side))
    prepare(2, 5)
    prepare(3, 6)
    prepare(4, 9)
    for b in range(2):
        rows = pl.ds(b, 64, stride=2)
        top, bottom = gate_matrix(g.at[10, 0][rows, :], g.at[10, 1][rows, :])
        mats[5, b * 64 : (b + 1) * 64, :] = top
        mats[5, 128 + b * 64 : 128 + (b + 1) * 64, :] = bottom
    load_perm.wait()
    blocks = []
    for j in range(16):
        block = jnp.int32(0)
        for v in range(1, 16):
            block = jnp.where(perm_ref[v] == j, v, block)
        blocks.append(block)
    nsend1.wait()
    qsrc[0] = nsrc[0] + nrecv[0]
    qsends = []
    for dx, dz in LO_STEPS:
        qsends.append(
            pltpu.make_async_remote_copy(
                src_ref=qsrc.at[0],
                dst_ref=qrecv.at[dx * 2 + dz],
                send_sem=qssem.at[dx * 2 + dz],
                recv_sem=qrsem.at[dx * 2 + dz],
                device_id=(hi, lo_peer(dx, dz)),
                device_id_type=MESH,
            )
        )

    send1.wait()
    gate_mid(1, lambda c: a1[c], t1, half(1 - side))

    put_rows(s2, left(mats[2], get_rows(t1)))
    side = bit_of(hi, SWAP_BITS[1])
    send2 = exchange(s2.at[:, half(1 - side), :], a2, 1, 1 << SWAP_BITS[1])
    send2.start()

    hear()
    signal(ready.at[2], hi_id(1 << SWAP_BITS[1]))

    @pl.when(z_at == 1)
    def _():
        signal(ready.at[0], (hi, lo_peer(0, 1)))

    @pl.when(z_at == 1)
    def _():
        for copy in qsends:
            copy.start()

    gate_mid(3, lambda c: s2[c, half(side), :], t2, half(side))
    send2.wait()

    gate_mid(3, lambda c: a2[c], t2, half(1 - side))

    put_rows(t1, left(mats[4], get_rows(t2)))
    data = jnp.concatenate(
        [jnp.concatenate([t1[c, 0:128, :], t1[c, 128:256, :]], axis=1) for c in range(2)], axis=0
    )
    y = left(mats[5], data)
    for c in range(2):
        for b in range(2):
            for t in range(2):
                base = c * 128 + b * 64
                u2[c, b, t * 8 : (t + 1) * 8] = y[
                    base : base + 64, t * 128 : (t + 1) * 128
                ].reshape(8, 8, 128)

    for j in range(16):
        for b in range(2):
            for c in range(2):
                stage[b, j, c] = u2[c, b, blocks[j]]
    sends = {}
    for b in range(2):
        for dx, dz in LO_STEPS:
            peer = lo_peer(dx, dz)
            sends[b, dx, dz] = pltpu.make_async_remote_copy(
                src_ref=stage.at[b, peer],
                dst_ref=recv.at[b, lo],
                send_sem=assem.at[b, dx * 2 + dz],
                recv_sem=arsem.at[b, dx * 2 + dz],
                device_id=(hi, peer),
                device_id_type=MESH,
            )

    def start(across):
        for b in range(2):
            for dx, dz in LO_STEPS:
                if dz == across:
                    sends[b, dx, dz].start()

    @pl.when(z_at == 0)
    def _():
        start(0)
        pl.semaphore_wait(ready.at[0], 1)
        for copy in qsends:
            copy.start()
        start(1)

    @pl.when(z_at == 1)
    def _():
        start(1)
        start(0)

    for b in range(2):
        recv[b, lo] = stage[b, lo]

    pl.semaphore_wait(ready.at[2], 1)

    @pl.when(z_bit == 1)
    def _():
        signal(ready.at[1], hi_id(Z_MASK))

    load_ga.wait()
    prepare(6, 13)
    prepare(7, 14)
    prod[0:128, :] = g[0, 0]
    prod[128:256, :] = g[0, 1]
    for gate in (3, 4, 7, 8, 11, 12, 15):
        top, bottom = gate_matrix(g[gate, 0], g[gate, 1])
        work[0:128, :] = top
        work[128:256, :] = bottom
        prod[...] = left(work[...], prod[...])
    top, bottom = gate_matrix(prod[0:128, :], prod[128:256, :])
    rmat[0:128, :] = top
    rmat[128:256, :] = bottom


    total = qsrc[0]
    for copy in qsends:
        copy.wait()
    for dx, dz in LO_STEPS:
        total = total + qrecv[dx * 2 + dz]
    qsrc[1] = total

    @pl.when(z_bit == 0)
    def _():
        pl.semaphore_wait(ready.at[1], 1)

    norm_sends = []
    for i, mask in enumerate(NORM_MASKS):
        copy = pltpu.make_async_remote_copy(
            src_ref=qsrc.at[1],
            dst_ref=nrecv.at[1 + i],
            send_sem=nssem.at[i],
            recv_sem=nrsem.at[i],
            device_id=hi_id(mask),
            device_id_type=MESH,
        )
        copy.start()
        norm_sends.append(copy)

    side = bit_of(hi, SWAP_BITS[2])

    def quarter(which):
        return pl.ds(pl.multiple_of(which * 64, 64), 64)

    sends3 = []
    for b in range(2):
        for dx, dz in LO_STEPS:
            sends[b, dx, dz].wait()
        data = jnp.concatenate(
            [recv[b, :, 0].reshape(128, 128), recv[b, :, 1].reshape(128, 128)], axis=0
        )
        y = left(mats[6], data)
        for c in range(2):
            f3[b, c] = y[c * 128 : (c + 1) * 128, :]
        copy = exchange(f3.at[b, :, quarter(1 - side), :], g3.at[b], 2 + b, 1 << SWAP_BITS[2])
        copy.start()
        sends3.append(copy)
    def low_bits(b, read):
        y = right(jnp.concatenate([read(0), read(1)], axis=1), rmat[...])
        for c in range(2):
            k3[c, pl.ds(b, 64, stride=2), :] = y[:, c * 128 : (c + 1) * 128]

    def finish(where):
        y = left(mats[7], jnp.concatenate([k3[0], k3[1]], axis=0))
        for c in range(2):
            out_ref[pl.ds(where * 256 + c, 128, stride=2), :] = y[c * 128 : (c + 1) * 128, :]

    for b in range(2):
        low_bits(b, lambda c: f3[b, c, quarter(side), :])
    finish(side)
    for b in range(2):
        sends3[b].wait()
        low_bits(b, lambda c: g3[b, c])
    finish(1 - side)
    total = qsrc[1]
    for copy in norm_sends:
        copy.wait()
    for i in range(len(NORM_MASKS)):
        total = total + nrecv[1 + i]
    mean_sq = jnp.sum(total, axis=1, keepdims=True) / count
    norm_ref[...] = jnp.broadcast_to(1.0 / jnp.sqrt(mean_sq + 1e-06), (1, 128))


def per_device(count, state, gates, remap_perm):
    rows = state.reshape(2, 256, 128).transpose(1, 0, 2).reshape(512, 128)
    vm = pltpu.VMEM
    dma = pltpu.SemaphoreType.DMA
    out, norm = pl.pallas_call(
        functools.partial(kernel, count),
        out_shape=(vm((512, 128), F32), vm((1, 128), F32)),
        in_specs=[
            pl.BlockSpec(memory_space=pl.ANY),
            pl.BlockSpec(memory_space=pl.ANY),
            pl.BlockSpec(memory_space=pl.ANY),
        ],
        out_specs=(
            pl.BlockSpec(memory_space=pltpu.VMEM),
            pl.BlockSpec(memory_space=pltpu.VMEM),
        ),
        scratch_shapes=[
            pltpu.SMEM((16,), jnp.int32),
            vm((512, 128), F32),
            vm((16, 2, 128, 128), F32),
            vm((8, 256, 768), BF16),
            vm((256, 768), BF16),
            vm((256, 768), BF16),
            vm((256, 128), F32),
            vm((2, 256, 128), F32),
            vm((2, 128, 128), F32),
            vm((2, 256, 128), F32),
            vm((2, 256, 128), F32),
            vm((2, 128, 128), F32),
            vm((2, 256, 128), F32),
            vm((2, 2, 16, 8, 128), F32),
            vm((2, 16, 2, 8, 128), F32),
            vm((2, 16, 2, 8, 128), F32),
            vm((2, 2, 128, 128), F32),
            vm((2, 2, 64, 128), F32),
            vm((2, 128, 128), F32),
            vm((1, 1, 128), F32),
            vm((32, 1, 128), F32),
            vm((2, 1, 128), F32),
            vm((16, 1, 128), F32),
            pltpu.SemaphoreType.REGULAR((4,)),
            pltpu.SemaphoreType.REGULAR((3,)),
            dma((5,)),
            dma((5,)),
            dma((5,)),
            dma((31,)),
            dma((31,)),
            dma((2, 16)),
            dma((2, 16)),
            dma((16,)),
            dma((16,)),
        ],
        compiler_params=pltpu.CompilerParams(collective_id=0, has_side_effects=True),
    )(remap_perm, rows, gates)
    return (out * norm).reshape(256, 2, 128).transpose(1, 0, 2).reshape(2, 32768)


def solution(mesh):
    devices = mesh.shape["hi"] * mesh.shape["lo"]
    in_specs = (P(None, ("hi", "lo")), P(), P())
    out_specs = P(None, ("hi", "lo"))
    return jax.shard_map(
        functools.partial(per_device, 2.0 * 32768 * devices),
        mesh=mesh,
        in_specs=in_specs,
        out_specs=out_specs,
        check_vma=False,
    )
```
